32 devices in a mesh: layer: 8 (over y, x, core), dp: 4 (over z).
Axes of the slice: x: 2, y: 2, z: 4, core: 2. Of those that a mesh axis runs over, the one named last changes fastest.
Arguments:
- resid_in: bfloat16 [4, 128, 3584], P(None, 'dp'), may hold values from -6 to 6
- resid_out: bfloat16 [4, 128, 3584], P(None, ('layer', 'dp')), may hold values from -4 to 4
- encoder: bfloat16 [2, 3584, 32768], P(None, None, ('layer', 'dp')), may hold values from -0.09375 to 0.09375
- enc_bias: float32 [2, 32768], P(None, ('layer', 'dp')), may hold values from -3 to 3
- decoder: bfloat16 [5, 32768, 3584], P(None, ('layer', 'dp')), may hold values from -0.046875 to 0.046875
- active: int32 [4, 4, 32], replicated, may hold values from 0 to 127, all different within a row
Outputs:
- recon: bfloat16 [4, 128, 3584], P(None, ('layer', 'dp'))
- grad_encoder: bfloat16 [2, 3584, 32768], P(None, None, ('layer', 'dp'))
- grad_bias: float32 [2, 32768], P(None, ('layer', 'dp'))
- grad_decoder: bfloat16 [5, 32768, 3584], P(None, ('layer', 'dp'))
The draws below stay inside these ranges and needn't reach their ends.
Inputs may be any that keep to these rules, and one draw needn't show every extreme that they name: Row active[l, n] lists 32 different blocks of layer l, active for tokens n * 32 to (n + 1) * 32 - 1; every block number appears in at least one row of active, counting the rows of all layers together (not necessarily in a row of every layer).
All inputs are finite; a program needn't handle non-finite values.
Results may differ from the reference program's by a relative error of at most 0.0059.
Values may be sent and summed in bfloat16 or wider, within the bound.
A program may use at most 192 MiB of HBM per device.

```python
import jax
import jax.numpy as jnp
from jax import lax

D = 3584
FEAT = 16384
BLOCK = 128
LAYERS = 4
PAIRS = 5
TOK_DEV = 32
TILES = 4
TOKENS = 128
ACTIVE = 32


def levels(stream_key, extent, cuts, low, top_value):
    def one(axis_at, parts):
        steps = jax.random.uniform(jax.random.fold_in(jax.random.fold_in(stream_key, 6), axis_at), (parts,), jnp.float32, low / len(cuts), top_value / len(cuts))
        return jnp.repeat(jnp.exp(steps), extent[axis_at] // parts).reshape((-1,) + (1,) * (len(extent) - axis_at - 1))

    loudness = one(*cuts[0])
    for cut in cuts[1:]:
        loudness = loudness * one(*cut)
    return loudness


def distinct(own_key, rows, number_of, top, lift):
    ranking = jax.random.permutation(jax.random.fold_in(own_key, 1), number_of)
    boost = ranking
    for power in range(3):
        boost = boost * boost // number_of
    boost = boost * lift // number_of
    tickets = jax.random.randint(jax.random.fold_in(own_key, 2), (rows, number_of), 0, 4096) + boost
    sure = jax.random.permutation(jax.random.fold_in(own_key, 3), rows)[jnp.arange(number_of) % rows]
    tickets = jnp.where(jnp.arange(rows)[:, None] == sure[None, :], 1 << 14, tickets)
    merit = tickets * number_of + jnp.arange(number_of)
    return lax.top_k(merit.astype(jnp.int32), top)[1].astype(jnp.int32)


def noise(rng, dims, scale, most, shards=(), kind=jnp.bfloat16):
    values = jax.random.normal(rng, dims, jnp.float32) * scale
    if len(shards) > 0:
        values = levels(rng, dims, shards, -0.22, 0.18) * values
    return jnp.clip(values, min=-most, max=most).astype(kind)


def setup_inputs(seed: int = 0) -> dict:
    arg_keys = jax.random.split(jax.random.key(seed), 7)
    resid_in = noise(arg_keys[0], (LAYERS, TOKENS, D), 1.0, 6.0, ((1, 4),))
    resid_out = noise(arg_keys[1], (LAYERS, TOKENS, D), 0.5, 4.0, ((1, 32),))
    encoder = noise(arg_keys[2], (2, D, 2 * FEAT), D ** -0.5, 0.09375, ((2, 32),))
    enc_bias = noise(arg_keys[3], (2, 2 * FEAT), 0.5, 3.0, ((1, 32),), jnp.float32)
    decoder = noise(arg_keys[4], (PAIRS, 2 * FEAT, D), FEAT ** -0.5, 0.046875, ((1, 32),))
    active = distinct(arg_keys[5], LAYERS * TILES, FEAT // BLOCK, ACTIVE, 4096).reshape((LAYERS, TILES, ACTIVE))
    return {"resid_in": resid_in, "resid_out": resid_out, "encoder": encoder, "enc_bias": enc_bias, "decoder": decoder, "active": active}


def pair_map(fold_side, pair_slot):
    if pair_slot >= LAYERS - fold_side:
        return 1, pair_slot - 1
    return 0, fold_side + pair_slot


def reference(resid_in, resid_out, encoder, enc_bias, decoder, active):
    block_ids = jnp.arange(FEAT // BLOCK, dtype=jnp.int32)
    decoded = jnp.zeros((LAYERS, TOKENS, D), jnp.float32)
    saved = []
    for fold_side in range(2):
        low_col = fold_side * FEAT
        high_col = low_col + FEAT
        layer_ids = [fold_side, LAYERS - 1 - fold_side]
        side_state = []
        for source_slot in range(2):
            layer_id = layer_ids[source_slot]
            inputs = resid_in[layer_id]
            pre_acts = jnp.dot(inputs, encoder[source_slot][:, low_col:high_col], preferred_element_type=jnp.float32) + enc_bias[source_slot, low_col:high_col]
            listed_hit = jnp.any(active[layer_id][:, :, None] == block_ids[None, None, :], axis=1).astype(jnp.float32)
            block_keep = jnp.repeat(jnp.repeat(listed_hit, TOK_DEV, axis=0), BLOCK, axis=1)
            positive = jnp.maximum(pre_acts, 0.0)
            feature_codes = (block_keep * positive * positive).astype(jnp.bfloat16)
            side_state.append((inputs, block_keep, positive, feature_codes))
        for pair_slot in range(PAIRS):
            source_slot, target_layer = pair_map(fold_side, pair_slot)
            decoded = decoded.at[target_layer].add(jnp.dot(side_state[source_slot][3], decoder[pair_slot][low_col:high_col], preferred_element_type=jnp.float32))
        saved.append(side_state)
    recon = decoded.astype(jnp.bfloat16)
    errors_all = (decoded - resid_out.astype(jnp.float32)).astype(jnp.bfloat16)
    enc_parts = []
    bias_parts = []
    dec_parts = []
    for fold_side in range(2):
        low_col = fold_side * FEAT
        high_col = low_col + FEAT
        back_codes = [jnp.zeros((TOKENS, FEAT), jnp.float32), jnp.zeros((TOKENS, FEAT), jnp.float32)]
        dec_side = []
        for pair_slot in range(PAIRS):
            source_slot, target_layer = pair_map(fold_side, pair_slot)
            codes_here = saved[fold_side][source_slot][3]
            dec_side.append(jnp.dot(codes_here.T, errors_all[target_layer], preferred_element_type=jnp.float32).astype(jnp.bfloat16))
            back_codes[source_slot] = back_codes[source_slot] + jnp.dot(errors_all[target_layer], decoder[pair_slot][low_col:high_col].T, preferred_element_type=jnp.float32)
        dec_parts.append(jnp.stack(dec_side))
        enc_side = []
        bias_side = []
        for source_slot in range(2):
            state = saved[fold_side][source_slot]
            back_pre = (back_codes[source_slot] * state[1] * (2.0 * state[2])).astype(jnp.bfloat16)
            enc_side.append(jnp.dot(state[0].T, back_pre, preferred_element_type=jnp.float32).astype(jnp.bfloat16))
            bias_side.append(jnp.sum(back_pre.astype(jnp.float32), axis=0))
        enc_parts.append(jnp.stack(enc_side))
        bias_parts.append(jnp.stack(bias_side))
    grad_encoder = jnp.concatenate(enc_parts, axis=2)
    grad_bias = jnp.concatenate(bias_parts, axis=1)
    grad_decoder = jnp.concatenate(dec_parts, axis=1)
    return recon, grad_encoder, grad_bias, grad_decoder
```

```python
import functools

import jax
import jax.numpy as jnp
from jax import lax
from jax.experimental import pallas as pl
from jax.experimental.pallas import tpu as pltpu
from jax.sharding import PartitionSpec as P

FEAT = 16384
BLOCK = 128
LAYERS = 4
MESH = pl.DeviceIdType.MESH
VMEM_LIMIT = 63 * 1000 * 1000


def remote(src, dst, send_sem, recv_sem, layer, dp):
    return pltpu.make_async_remote_copy(
        src_ref=src,
        dst_ref=dst,
        send_sem=send_sem,
        recv_sem=recv_sem,
        device_id=(layer, dp),
        device_id_type=MESH,
    )


def greet(layer, dp, dp_count, bits):
    barrier = pltpu.get_barrier_semaphore()
    for hop in range(1, dp_count):
        pl.semaphore_signal(
            barrier, inc=1, device_id=(layer, lax.rem(dp + hop, dp_count)), device_id_type=MESH
        )
    for bit in bits:
        pl.semaphore_signal(
            barrier, inc=1, device_id=(flip(layer, bit), dp), device_id_type=MESH
        )
    return barrier, dp_count - 1 + len(bits)


def bit_of(value, bit):
    return (value // (1 << bit)) % 2


def flip(value, bit):
    return value + (1 - 2 * bit_of(value, bit)) * (1 << bit)


def spread_bits(base, bits, count):
    for place, bit in enumerate(bits):
        base = base + (((count >> place) & 1) - bit_of(base, bit)) * (1 << bit)
    return base


def gather_kernel(layer_count, dp_count, x_ref, g_ref, hold, send_sem, recv_sem, near_sem, out_sem):
    layer, dp = lax.axis_index("layer"), lax.axis_index("dp")
    group = layer_count // 2
    halves = x_ref.shape[1]
    nbits = group.bit_length() - 1
    side = layer // group
    bits = list(range(nbits - 1, -1, -1))
    barrier, greeted = greet(layer, dp, dp_count, bits)
    mine = layer % group
    near = []
    for slot in range(2):
        layer_id = side + slot * (LAYERS - 1 - 2 * side)
        copy = pltpu.make_async_copy(
            x_ref.at[layer_id], hold.at[slot, dp], near_sem.at[slot]
        )
        copy.start()
        near.append(copy)
    pl.semaphore_wait(barrier, greeted)

    def piece(ref, source, index):
        return ref.at[index // halves, source, index % halves]

    copies = {}
    my_slot = mine // halves
    own = x_ref.at[side + my_slot * (LAYERS - 1 - 2 * side), mine % halves]
    for hop in range(1, dp_count):
        copies[hop, 0] = remote(
            own, piece(hold, dp, mine), send_sem.at[hop, 0], recv_sem.at[hop, 0],
            layer, lax.rem(dp + hop, dp_count),
        )
        copies[hop, 0].start()
    for step, bit in enumerate(bits):
        for hop in range(1, dp_count):
            source = lax.rem(dp + dp_count - hop, dp_count)
            arrived = [0] if step == 0 else range(1 << (step - 1), 1 << step)
            for index in arrived:
                copies[hop, index].wait_recv()
            for count in range(1 << step):
                index = spread_bits(mine, bits[:step], count)
                slot = (1 << step) + count
                block = piece(hold, source, index)
                copies[hop, slot] = remote(
                    block, block, send_sem.at[hop, slot], recv_sem.at[hop, slot],
                    flip(layer, bit), dp,
                )
                copies[hop, slot].start()
    for hop in range(1, dp_count):
        for index in range(group // 2, group):
            copies[hop, index].wait_recv()
    for copy in near:
        copy.wait()
    out = pltpu.make_async_copy(hold, g_ref, out_sem)
    out.start()
    for copy in copies.values():
        copy.wait_send()
    out.wait()


def gather_inputs(resid_in, layer_count, dp_count):
    layers, tok_dev, width = resid_in.shape
    group = layer_count // 2
    halves = group // 2
    rows = tok_dev // halves
    x = resid_in.reshape(layers, halves, rows, width)
    shape = (2, dp_count, halves, rows, width)
    out = pl.pallas_call(
        functools.partial(gather_kernel, layer_count, dp_count),
        out_shape=jax.ShapeDtypeStruct(shape, resid_in.dtype),
        in_specs=[pl.BlockSpec(memory_space=pltpu.VMEM)],
        out_specs=pl.BlockSpec(memory_space=pl.ANY),
        scratch_shapes=[
            pltpu.VMEM(shape, resid_in.dtype),
            pltpu.SemaphoreType.DMA((dp_count, group)),
            pltpu.SemaphoreType.DMA((dp_count, group)),
            pltpu.SemaphoreType.DMA((2,)),
            pltpu.SemaphoreType.DMA,
        ],
        compiler_params=pltpu.CompilerParams(
            collective_id=0, has_side_effects=True, vmem_limit_bytes=32 * 1000 * 1000
        ),
        name="gather_inputs",
    )(x)
    return out.reshape(2, dp_count * tok_dev, width)


def exchange_kernel(
    layer_count, dp_count, codes_ref, dec_ref, target_ref, recon_ref, err_out,
    weights, part, arrivals, err, zsend, zrecv, zall, acc,
    load_sem, rs_send, rs_recv, z_send, z_recv, g_send, g_recv, ag_send, ag_recv, out_sem,
):
    layer, dp = lax.axis_index("layer"), lax.axis_index("dp")
    nbits = layer_count.bit_length() - 1
    side = layer // (layer_count // 2)
    pairs, width = dec_ref.shape[0], dec_ref.shape[2]
    rows = part.shape[2]
    share = target_ref.shape[1]
    f32, bf16 = jnp.float32, jnp.bfloat16
    loads = []
    for pair in range(pairs):
        loads.append(pltpu.make_async_copy(dec_ref.at[pair], weights.at[pair], load_sem.at[pair]))
        loads[-1].start()
    barrier, greeted = greet(layer, dp, dp_count, range(nbits))
    tile = 512 if width % 512 == 0 else 128
    orders = []
    for target in range(LAYERS):
        upper = list(range(nbits - 1, 0, -1))
        orders.append([0] + (upper if target % 2 else upper[::-1]))
    copies = {}

    def add_pair(slot, pair, fresh):
        def body(step, carry):
            columns = pl.ds(pl.multiple_of(step * tile, tile), tile)
            value = jnp.dot(
                codes_ref[slot], weights[pair, :, columns], preferred_element_type=f32
            )
            if fresh:
                acc[:, columns] = value
            else:
                acc[:, columns] += value
            return carry

        lax.fori_loop(0, width // tile, body, 0)

    def wait_load(pair):
        loads[pair].wait()

    def decode(target):
        has_first = (target >= side) if target == 0 else None

        def first():
            add_pair(0, target - side, True)

        if target == 0:
            pl.when(side == 0)(first)

            @pl.when(side != 0)
            def _():
                acc[...] = jnp.zeros_like(acc)
        else:
            first()
        if target >= LAYERS - 2:
            def second():
                add_pair(1, target + 1, False)

            if target == LAYERS - 2:
                pl.when(side == 1)(second)
            else:
                second()
        part[target] = acc[...].reshape(part.shape[1:]).astype(bf16)

    def halve_send(target, stage):
        order = orders[target]
        bit = order[stage]
        partner = flip(layer, bit)
        rest = order[stage + 1:]
        for count in range(1 << len(rest)):
            block = spread_bits(partner, rest, count)
            slot = (1 << len(rest)) - 1 + count
            copy = remote(
                part.at[target, block], arrivals.at[target, slot],
                rs_send.at[target, slot], rs_recv.at[target, slot], partner, dp,
            )
            copy.start()
            copies["rs", target, slot] = copy

    def halve_take(target, stage):
        order = orders[target]
        rest = order[stage + 1:]
        for count in range(1 << len(rest)):
            slot = (1 << len(rest)) - 1 + count
            copies["rs", target, slot].wait_recv()
            block = spread_bits(layer, rest, count)
            total = part[target, block].astype(f32) + arrivals[target, slot].astype(f32)
            if stage < nbits - 1:
                part[target, block] = total.astype(bf16)
            else:
                for place in range(dp_count):
                    zsend[target, place] = total[place * share:(place + 1) * share].astype(bf16)

    def peers():
        for hop in range(1, dp_count):
            yield hop, lax.rem(dp + hop, dp_count)

    def swap_send(target):
        for hop, peer in peers():
            copy = remote(
                zsend.at[target, peer], zrecv.at[target, hop],
                z_send.at[target, hop], z_recv.at[target, hop], layer, peer,
            )
            copy.start()
            copies["z", target, hop] = copy

    def finish(target):
        total = zsend[target, dp].astype(f32)
        for hop in range(1, dp_count):
            copies["z", target, hop].wait_recv()
            total = total + zrecv[target, hop].astype(f32)
        recon_ref[target] = total.astype(bf16)
        zall[target, dp] = (total - target_ref[target].astype(f32)).astype(bf16)
        for hop, peer in peers():
            copy = remote(
                zall.at[target, dp], zall.at[target, dp],
                g_send.at[target, hop], g_recv.at[target, hop], layer, peer,
            )
            copy.start()
            copies["g", target, hop] = copy

    def assemble(target):
        for hop in range(1, dp_count):
            copies["g", target, hop].wait_recv()
        err[target, layer] = jnp.concatenate(
            [zall[target, place].astype(f32) for place in range(dp_count)], axis=0
        ).astype(bf16)

    def double_send(target, step):
        order = orders[target][::-1]
        bit = order[step]
        for count in range(1 << step):
            block = spread_bits(layer, order[:step], count)
            slot = (1 << step) - 1 + count
            copy = remote(
                err.at[target, block], err.at[target, block],
                ag_send.at[target, slot], ag_recv.at[target, slot], flip(layer, bit), dp,
            )
            copy.start()
            copies["ag", target, slot] = copy

    def double_take(target, step):
        for count in range(1 << step):
            copies["ag", target, (1 << step) - 1 + count].wait_recv()

    def run(target, stage):
        if stage == 0:
            decode(target)
            if target == 0:
                pl.semaphore_wait(barrier, greeted)
            halve_send(target, 0)
        elif stage <= nbits:
            halve_take(target, stage - 1)
            if stage < nbits:
                halve_send(target, stage)
            else:
                swap_send(target)
        elif stage == nbits + 1:
            finish(target)
        elif stage == nbits + 2:
            assemble(target)
            double_send(target, 0)
        else:
            step = stage - nbits - 3
            double_take(target, step)
            if step < nbits - 1:
                double_send(target, step + 1)
            else:
                copy = pltpu.make_async_copy(err.at[target], err_out.at[target], out_sem.at[target])
                copy.start()
                copies["out", target, 0] = copy

    for load in loads:
        load.wait()
    last = 2 * nbits + 2
    for wave in range(last + LAYERS):
        for target in range(LAYERS - 1, -1, -1):
            if 0 <= wave - target <= last:
                run(target, wave - target)
    for key, copy in copies.items():
        if key[0] == "out":
            copy.wait()
        else:
            copy.wait_send()


def exchange(codes, decoder, targets, layer_count, dp_count):
    tokens = codes.shape[1]
    pairs, local_width, width = decoder.shape
    rows = tokens // layer_count
    share = rows // dp_count
    bf16 = jnp.bfloat16
    dma = pltpu.SemaphoreType.DMA
    recon, errors = pl.pallas_call(
        functools.partial(exchange_kernel, layer_count, dp_count),
        out_shape=[
            jax.ShapeDtypeStruct((LAYERS, share, width), bf16),
            jax.ShapeDtypeStruct((LAYERS, layer_count, rows, width), bf16),
        ],
        in_specs=[
            pl.BlockSpec(memory_space=pltpu.VMEM),
            pl.BlockSpec(memory_space=pl.ANY),
            pl.BlockSpec(memory_space=pltpu.VMEM),
        ],
        out_specs=[
            pl.BlockSpec(memory_space=pltpu.VMEM),
            pl.BlockSpec(memory_space=pl.ANY),
        ],
        scratch_shapes=[
            pltpu.VMEM((pairs, local_width, width), bf16),
            pltpu.VMEM((LAYERS, layer_count, rows, width), bf16),
            pltpu.VMEM((LAYERS, layer_count - 1, rows, width), bf16),
            pltpu.VMEM((LAYERS, layer_count, rows, width), bf16),
            pltpu.VMEM((LAYERS, dp_count, share, width), bf16),
            pltpu.VMEM((LAYERS, dp_count, share, width), bf16),
            pltpu.VMEM((LAYERS, dp_count, share, width), bf16),
            pltpu.VMEM((tokens, width), jnp.float32),
            dma((pairs,)),
            dma((LAYERS, layer_count - 1)),
            dma((LAYERS, layer_count - 1)),
            dma((LAYERS, dp_count)),
            dma((LAYERS, dp_count)),
            dma((LAYERS, dp_count)),
            dma((LAYERS, dp_count)),
            dma((LAYERS, layer_count - 1)),
            dma((LAYERS, layer_count - 1)),
            dma((LAYERS,)),
        ],
        compiler_params=pltpu.CompilerParams(
            collective_id=1, has_side_effects=True, vmem_limit_bytes=VMEM_LIMIT
        ),
        name="decode_exchange",
    )(codes, decoder, targets)
    return recon, errors.reshape(LAYERS, tokens, width)


def per_device(resid_in, resid_out, encoder, enc_bias, decoder, active):
    tok_dev = resid_in.shape[1]
    local_width = encoder.shape[2]
    layer_count = lax.axis_size("layer")
    dp_count = lax.axis_size("dp")
    device_rank = lax.axis_index("layer") * dp_count + lax.axis_index("dp")
    first_column = device_rank * local_width
    fold_side = first_column // FEAT
    offset = first_column - fold_side * FEAT
    layer_ids = [fold_side, LAYERS - 1 - fold_side]
    inputs = gather_inputs(resid_in, layer_count, dp_count)
    tokens = inputs.shape[1]
    pre_acts = (
        jnp.einsum("krd,kdf->krf", inputs, encoder, preferred_element_type=jnp.float32)
        + enc_bias[:, None, :]
    )
    block_ids = offset // BLOCK + jnp.arange(local_width // BLOCK, dtype=jnp.int32)
    block_masks = []
    for layer_id in layer_ids:
        listed = lax.dynamic_index_in_dim(active, layer_id, 0, keepdims=False)
        listed_hit = jnp.any(listed[:, :, None] == block_ids[None, None, :], axis=1).astype(
            jnp.float32
        )
        spread = jnp.broadcast_to(
            listed_hit[:, None, :, None], (listed_hit.shape[0], tok_dev, listed_hit.shape[1], BLOCK)
        )
        block_masks.append(spread.reshape(tokens, local_width))
    block_keep = jnp.stack(block_masks)
    positive = jnp.maximum(pre_acts, 0.0)
    feature_codes = (block_keep * positive * positive).astype(jnp.bfloat16)
    recon, errors_all = exchange(feature_codes, decoder, resid_out, layer_count, dp_count)
    pair_table = []
    for pair_slot in range(decoder.shape[0]):
        second = pair_slot >= LAYERS - fold_side
        pair_table.append(
            (second.astype(jnp.int32), jnp.where(second, pair_slot - 1, fold_side + pair_slot))
        )
    grad_parts = []
    back_codes = jnp.zeros((2, tokens, local_width), jnp.float32)
    for pair_slot in range(decoder.shape[0]):
        source_slot, target_layer = pair_table[pair_slot]
        source_codes = lax.dynamic_index_in_dim(feature_codes, source_slot, 0, keepdims=False)
        target_errors = lax.dynamic_index_in_dim(errors_all, target_layer, 0, keepdims=False)
        grad_parts.append(
            lax.dot_general(
                source_codes,
                target_errors,
                (((0,), (0,)), ((), ())),
                preferred_element_type=jnp.float32,
            ).astype(jnp.bfloat16)
        )
        pulled = lax.dot_general(
            target_errors,
            decoder[pair_slot],
            (((1,), (1,)), ((), ())),
            preferred_element_type=jnp.float32,
        )
        current = lax.dynamic_index_in_dim(back_codes, source_slot, 0, keepdims=False)
        back_codes = lax.dynamic_update_index_in_dim(back_codes, current + pulled, source_slot, 0)
    grad_decoder = jnp.stack(grad_parts)
    back_pre = (back_codes * block_keep * (2.0 * positive)).astype(jnp.bfloat16)
    grad_encoder = jnp.einsum(
        "krd,krf->kdf", inputs, back_pre, preferred_element_type=jnp.float32
    ).astype(jnp.bfloat16)
    grad_bias = jnp.sum(back_pre.astype(jnp.float32), axis=1)
    return (recon, grad_encoder, grad_bias, grad_decoder)


def solution(mesh):
    in_specs = (
        P(None, "dp", None),
        P(None, ("layer", "dp"), None),
        P(None, None, ("layer", "dp")),
        P(None, ("layer", "dp")),
        P(None, ("layer", "dp"), None),
        P(),
    )
    out_specs = (
        P(None, ("layer", "dp"), None),
        P(None, None, ("layer", "dp")),
        P(None, ("layer", "dp")),
        P(None, ("layer", "dp"), None),
    )
    return jax.shard_map(
        per_device, mesh=mesh, in_specs=in_specs, out_specs=out_specs, check_vma=False
    )
```

```python
import functools

import jax
import jax.numpy as jnp
from jax import lax
from jax.experimental import pallas as pl
from jax.experimental.pallas import tpu as pltpu
from jax.sharding import PartitionSpec as P

FEAT = 16384
BLOCK = 128
LAYERS = 4
MESH = pl.DeviceIdType.MESH
VMEM_LIMIT = 63 * 1000 * 1000


def remote(src, dst, send_sem, recv_sem, layer, dp):
    return pltpu.make_async_remote_copy(
        src_ref=src,
        dst_ref=dst,
        send_sem=send_sem,
        recv_sem=recv_sem,
        device_id=(layer, dp),
        device_id_type=MESH,
    )


def greet(layer, dp, dp_count, bits):
    barrier = pltpu.get_barrier_semaphore()
    for hop in range(1, dp_count):
        pl.semaphore_signal(
            barrier, inc=1, device_id=(layer, lax.rem(dp + hop, dp_count)), device_id_type=MESH
        )
    for bit in bits:
        pl.semaphore_signal(
            barrier, inc=1, device_id=(flip(layer, bit), dp), device_id_type=MESH
        )
    return barrier, dp_count - 1 + len(bits)


def bit_of(value, bit):
    return (value // (1 << bit)) % 2


def flip(value, bit):
    return value + (1 - 2 * bit_of(value, bit)) * (1 << bit)


def spread_bits(base, bits, count):
    for place, bit in enumerate(bits):
        base = base + (((count >> place) & 1) - bit_of(base, bit)) * (1 << bit)
    return base


def gather_kernel(layer_count, dp_count, x_ref, g_ref, hold, send_sem, recv_sem, near_sem, out_sem):
    layer, dp = lax.axis_index("layer"), lax.axis_index("dp")
    group = layer_count // 2
    halves = x_ref.shape[1]
    nbits = group.bit_length() - 1
    side = layer // group
    bits = list(range(nbits - 1, -1, -1))
    barrier, greeted = greet(layer, dp, dp_count, bits)
    mine = layer % group
    near = []
    for slot in range(2):
        layer_id = side + slot * (LAYERS - 1 - 2 * side)
        copy = pltpu.make_async_copy(
            x_ref.at[layer_id], hold.at[slot, dp], near_sem.at[slot]
        )
        copy.start()
        near.append(copy)
    pl.semaphore_wait(barrier, greeted)

    def piece(ref, source, index):
        return ref.at[index // halves, source, index % halves]

    copies = {}
    my_slot = mine // halves
    own = x_ref.at[side + my_slot * (LAYERS - 1 - 2 * side), mine % halves]
    for hop in range(1, dp_count):
        copies[hop, 0] = remote(
            own, piece(hold, dp, mine), send_sem.at[hop, 0], recv_sem.at[hop, 0],
            layer, lax.rem(dp + hop, dp_count),
        )
        copies[hop, 0].start()
    for step, bit in enumerate(bits):
        for hop in range(1, dp_count):
            source = lax.rem(dp + dp_count - hop, dp_count)
            arrived = [0] if step == 0 else range(1 << (step - 1), 1 << step)
            for index in arrived:
                copies[hop, index].wait_recv()
            for count in range(1 << step):
                index = spread_bits(mine, bits[:step], count)
                slot = (1 << step) + count
                block = piece(hold, source, index)
                copies[hop, slot] = remote(
                    block, block, send_sem.at[hop, slot], recv_sem.at[hop, slot],
                    flip(layer, bit), dp,
                )
                copies[hop, slot].start()
    for hop in range(1, dp_count):
        for index in range(group // 2, group):
            copies[hop, index].wait_recv()
    for copy in near:
        copy.wait()
    out = pltpu.make_async_copy(hold, g_ref, out_sem)
    out.start()
    for copy in copies.values():
        copy.wait_send()
    out.wait()


def gather_inputs(resid_in, layer_count, dp_count):
    layers, tok_dev, width = resid_in.shape
    group = layer_count // 2
    halves = group // 2
    rows = tok_dev // halves
    x = resid_in.reshape(layers, halves, rows, width)
    shape = (2, dp_count, halves, rows, width)
    out = pl.pallas_call(
        functools.partial(gather_kernel, layer_count, dp_count),
        out_shape=jax.ShapeDtypeStruct(shape, resid_in.dtype),
        in_specs=[pl.BlockSpec(memory_space=pltpu.VMEM)],
        out_specs=pl.BlockSpec(memory_space=pl.ANY),
        scratch_shapes=[
            pltpu.VMEM(shape, resid_in.dtype),
            pltpu.SemaphoreType.DMA((dp_count, group)),
            pltpu.SemaphoreType.DMA((dp_count, group)),
            pltpu.SemaphoreType.DMA((2,)),
            pltpu.SemaphoreType.DMA,
        ],
        compiler_params=pltpu.CompilerParams(
            collective_id=0, has_side_effects=True, vmem_limit_bytes=32 * 1000 * 1000
        ),
        name="gather_inputs",
    )(x)
    return out.reshape(2, dp_count * tok_dev, width)


def exchange_kernel(
    layer_count, dp_count, codes_ref, dec_ref, target_ref, recon_ref, err_out, back_ref,
    weights, part, arrivals, err, zsend, zrecv, zall, acc,
    load_sem, rs_send, rs_recv, z_send, z_recv, g_send, g_recv, ag_send, ag_recv, out_sem,
):
    layer, dp = lax.axis_index("layer"), lax.axis_index("dp")
    nbits = layer_count.bit_length() - 1
    side = layer // (layer_count // 2)
    pairs, width = dec_ref.shape[0], dec_ref.shape[2]
    rows = part.shape[2]
    share = target_ref.shape[1]
    f32, bf16 = jnp.float32, jnp.bfloat16

    def load(pair):
        return pltpu.make_async_copy(dec_ref.at[pair], weights.at[pair], load_sem.at[pair])

    for pair in range(LAYERS - 1):
        load(pair).start()
    for pair in range(LAYERS - 1, pairs):
        load(pair).start()
    barrier, greeted = greet(layer, dp, dp_count, range(nbits))
    tile = 512 if width % 512 == 0 else 128
    orders = []
    for target in range(LAYERS):
        upper = list(range(nbits - 1, 0, -1))
        orders.append([0] + (upper if target % 2 else upper[::-1]))
    copies = {}

    def add_pair(slot, pair, fresh):
        load(pair).wait()

        def body(step, carry):
            columns = pl.ds(pl.multiple_of(step * tile, tile), tile)
            value = jnp.dot(
                codes_ref[slot], weights[pair, :, columns], preferred_element_type=f32
            )
            if fresh:
                acc[:, columns] = value
            else:
                acc[:, columns] += value
            return carry

        lax.fori_loop(0, width // tile, body, 0)

    def pull_pair(target, slot, pair, fresh):
        deep = min(256, weights.shape[1])

        def body(step, carry):
            features = pl.ds(pl.multiple_of(step * deep, deep), deep)
            value = lax.dot_general(
                err[target].reshape(acc.shape),
                weights[pair, features, :],
                (((1,), (1,)), ((), ())),
                preferred_element_type=f32,
            )
            if fresh:
                back_ref[slot, :, features] = value
            else:
                back_ref[slot, :, features] += value
            return carry

        lax.fori_loop(0, weights.shape[1] // deep, body, 0)

    def pull(target):
        if target == 0:
            pl.when(side == 0)(lambda: pull_pair(0, 0, 0, True))
        elif target == 1:
            pl.when(side == 0)(lambda: pull_pair(1, 0, 1, False))
            pl.when(side == 1)(lambda: pull_pair(1, 0, 0, True))
        else:
            pull_pair(target, 0, target - side, False)
        if target == LAYERS - 2:
            pl.when(side == 1)(lambda: pull_pair(target, 1, target + 1, True))
        elif target == LAYERS - 1:
            pl.when(side == 1)(lambda: pull_pair(target, 1, target + 1, False))
            pl.when(side == 0)(lambda: pull_pair(target, 1, target + 1, True))

    def decode(target):
        def first():
            add_pair(0, target - side, True)

        if target == 0:
            pl.when(side == 0)(first)

            @pl.when(side != 0)
            def _():
                acc[...] = jnp.zeros_like(acc)
        else:
            first()
        if target >= LAYERS - 2:
            def second():
                add_pair(1, target + 1, False)

            if target == LAYERS - 2:
                pl.when(side == 1)(second)
            else:
                second()
        part[target] = acc[...].reshape(part.shape[1:]).astype(bf16)

    def halve_send(target, stage):
        order = orders[target]
        bit = order[stage]
        partner = flip(layer, bit)
        rest = order[stage + 1:]
        for count in range(1 << len(rest)):
            block = spread_bits(partner, rest, count)
            slot = (1 << len(rest)) - 1 + count
            copy = remote(
                part.at[target, block], arrivals.at[target, slot],
                rs_send.at[target, slot], rs_recv.at[target, slot], partner, dp,
            )
            copy.start()
            copies["rs", target, slot] = copy

    def halve_take(target, stage):
        order = orders[target]
        rest = order[stage + 1:]
        for count in range(1 << len(rest)):
            slot = (1 << len(rest)) - 1 + count
            copies["rs", target, slot].wait_recv()
            block = spread_bits(layer, rest, count)
            total = part[target, block].astype(f32) + arrivals[target, slot].astype(f32)
            if stage < nbits - 1:
                part[target, block] = total.astype(bf16)
            else:
                for place in range(dp_count):
                    zsend[target, place] = total[place * share:(place + 1) * share].astype(bf16)

    def peers():
        for hop in range(1, dp_count):
            yield hop, lax.rem(dp + hop, dp_count)

    def swap_send(target):
        for hop, peer in peers():
            copy = remote(
                zsend.at[target, peer], zrecv.at[target, hop],
                z_send.at[target, hop], z_recv.at[target, hop], layer, peer,
            )
            copy.start()
            copies["z", target, hop] = copy

    def finish(target):
        total = zsend[target, dp].astype(f32)
        for hop in range(1, dp_count):
            copies["z", target, hop].wait_recv()
            total = total + zrecv[target, hop].astype(f32)
        recon_ref[target] = total.astype(bf16)
        zall[target, dp] = (total - target_ref[target].astype(f32)).astype(bf16)
        for hop, peer in peers():
            copy = remote(
                zall.at[target, dp], zall.at[target, dp],
                g_send.at[target, hop], g_recv.at[target, hop], layer, peer,
            )
            copy.start()
            copies["g", target, hop] = copy

    def assemble(target):
        for hop in range(1, dp_count):
            copies["g", target, hop].wait_recv()
        err[target, layer] = jnp.concatenate(
            [zall[target, place].astype(f32) for place in range(dp_count)], axis=0
        ).astype(bf16)

    def double_send(target, step):
        order = orders[target][::-1]
        bit = order[step]
        for count in range(1 << step):
            block = spread_bits(layer, order[:step], count)
            slot = (1 << step) - 1 + count
            copy = remote(
                err.at[target, block], err.at[target, block],
                ag_send.at[target, slot], ag_recv.at[target, slot], flip(layer, bit), dp,
            )
            copy.start()
            copies["ag", target, slot] = copy

    def double_take(target, step):
        for count in range(1 << step):
            copies["ag", target, (1 << step) - 1 + count].wait_recv()

    def run(target, stage):
        if stage == 0:
            decode(target)
            if target == 0:
                pl.semaphore_wait(barrier, greeted)
            halve_send(target, 0)
        elif stage <= nbits:
            halve_take(target, stage - 1)
            if stage < nbits:
                halve_send(target, stage)
            else:
                swap_send(target)
        elif stage == nbits + 1:
            finish(target)
        elif stage == nbits + 2:
            assemble(target)
            double_send(target, 0)
        else:
            step = stage - nbits - 3
            double_take(target, step)
            if step < nbits - 1:
                double_send(target, step + 1)
            else:
                copy = pltpu.make_async_copy(err.at[target], err_out.at[target], out_sem.at[target])
                copy.start()
                copies["out", target, 0] = copy

    last = 2 * nbits + 2
    for wave in range(last + LAYERS):
        for target in range(LAYERS - 1, -1, -1):
            if 0 <= wave - target <= last:
                run(target, wave - target)
        if 0 <= wave - last < LAYERS:
            pull(wave - last)
    for key, copy in copies.items():
        if key[0] == "out":
            copy.wait()
        else:
            copy.wait_send()


def exchange(codes, decoder, targets, layer_count, dp_count):
    tokens = codes.shape[1]
    pairs, local_width, width = decoder.shape
    rows = tokens // layer_count
    share = rows // dp_count
    bf16 = jnp.bfloat16
    dma = pltpu.SemaphoreType.DMA
    recon, errors, back = pl.pallas_call(
        functools.partial(exchange_kernel, layer_count, dp_count),
        out_shape=[
            jax.ShapeDtypeStruct((LAYERS, share, width), bf16),
            jax.ShapeDtypeStruct((LAYERS, layer_count, rows, width), bf16),
            jax.ShapeDtypeStruct((2, tokens, local_width), jnp.float32),
        ],
        in_specs=[
            pl.BlockSpec(memory_space=pltpu.VMEM),
            pl.BlockSpec(memory_space=pl.ANY),
            pl.BlockSpec(memory_space=pltpu.VMEM),
        ],
        out_specs=[
            pl.BlockSpec(memory_space=pltpu.VMEM),
            pl.BlockSpec(memory_space=pl.ANY),
            pl.BlockSpec(memory_space=pltpu.VMEM),
        ],
        scratch_shapes=[
            pltpu.VMEM((pairs, local_width, width), bf16),
            pltpu.VMEM((LAYERS, layer_count, rows, width), bf16),
            pltpu.VMEM((LAYERS, layer_count - 1, rows, width), bf16),
            pltpu.VMEM((LAYERS, layer_count, rows, width), bf16),
            pltpu.VMEM((LAYERS, dp_count, share, width), bf16),
            pltpu.VMEM((LAYERS, dp_count, share, width), bf16),
            pltpu.VMEM((LAYERS, dp_count, share, width), bf16),
            pltpu.VMEM((tokens, width), jnp.float32),
            dma((pairs,)),
            dma((LAYERS, layer_count - 1)),
            dma((LAYERS, layer_count - 1)),
            dma((LAYERS, dp_count)),
            dma((LAYERS, dp_count)),
            dma((LAYERS, dp_count)),
            dma((LAYERS, dp_count)),
            dma((LAYERS, layer_count - 1)),
            dma((LAYERS, layer_count - 1)),
            dma((LAYERS,)),
        ],
        compiler_params=pltpu.CompilerParams(
            collective_id=1, has_side_effects=True, vmem_limit_bytes=VMEM_LIMIT
        ),
        name="decode_exchange",
    )(codes, decoder, targets)
    return recon, errors.reshape(LAYERS, tokens, width), back


def grad_decoder_kernel(source_ref, target_ref, codes_ref, err_ref, out_ref):
    width = err_ref.shape[2]
    tile = 512 if width % 512 == 0 else 128
    for first in range(0, width, tile):
        out_ref[0, :, first:first + tile] = lax.dot_general(
            codes_ref[0],
            err_ref[0, :, first:first + tile],
            (((0,), (0,)), ((), ())),
            preferred_element_type=jnp.float32,
        ).astype(out_ref.dtype)


def decoder_grad(codes, errors, sources, targets, pairs):
    tokens, local_width = codes.shape[1:]
    width = errors.shape[2]
    deep = min(256, local_width)
    return pl.pallas_call(
        grad_decoder_kernel,
        out_shape=jax.ShapeDtypeStruct((pairs, local_width, width), jnp.bfloat16),
        grid_spec=pltpu.PrefetchScalarGridSpec(
            num_scalar_prefetch=2,
            grid=(pairs, local_width // deep),
            in_specs=[
                pl.BlockSpec((1, tokens, deep), lambda p, f, src, tgt: (src[p], 0, f)),
                pl.BlockSpec((1, tokens, width), lambda p, f, src, tgt: (tgt[p], 0, 0)),
            ],
            out_specs=pl.BlockSpec((1, deep, width), lambda p, f, src, tgt: (p, f, 0)),
        ),
        name="decoder_grad",
    )(sources, targets, codes, errors)


def grad_encoder_kernel(x_ref, back_ref, keep_ref, positive_ref, grad_ref, bias_ref, back_pre):
    @pl.when(pl.program_id(1) == 0)
    def _():
        value = (back_ref[0] * keep_ref[0] * (2.0 * positive_ref[0])).astype(jnp.bfloat16)
        back_pre[...] = value
        bias_ref[0] = jnp.sum(value.astype(jnp.float32), axis=0, keepdims=True)

    grad_ref[0] = lax.dot_general(
        x_ref[0], back_pre[...], (((0,), (0,)), ((), ())), preferred_element_type=jnp.float32
    ).astype(grad_ref.dtype)


def encoder_grad(inputs, back, keep, positive):
    slots, tokens, width = inputs.shape
    local_width = back.shape[2]
    tile = 512 if width % 512 == 0 else 128
    whole = pl.BlockSpec((1, tokens, local_width), lambda k, d: (k, 0, 0))
    grad, bias = pl.pallas_call(
        grad_encoder_kernel,
        out_shape=[
            jax.ShapeDtypeStruct((slots, width, local_width), jnp.bfloat16),
            jax.ShapeDtypeStruct((slots, 1, local_width), jnp.float32),
        ],
        grid=(slots, width // tile),
        in_specs=[pl.BlockSpec((1, tokens, tile), lambda k, d: (k, 0, d)), whole, whole, whole],
        out_specs=[
            pl.BlockSpec((1, tile, local_width), lambda k, d: (k, d, 0)),
            pl.BlockSpec((1, 1, local_width), lambda k, d: (k, 0, 0)),
        ],
        scratch_shapes=[pltpu.VMEM((tokens, local_width), jnp.bfloat16)],
        name="encoder_grad",
    )(inputs, back, keep, positive)
    return grad, bias.reshape(slots, local_width)


def per_device(resid_in, resid_out, encoder, enc_bias, decoder, active):
    tok_dev = resid_in.shape[1]
    local_width = encoder.shape[2]
    layer_count = lax.axis_size("layer")
    dp_count = lax.axis_size("dp")
    device_rank = lax.axis_index("layer") * dp_count + lax.axis_index("dp")
    first_column = device_rank * local_width
    fold_side = first_column // FEAT
    offset = first_column - fold_side * FEAT
    layer_ids = [fold_side, LAYERS - 1 - fold_side]
    inputs = gather_inputs(resid_in, layer_count, dp_count)
    tokens = inputs.shape[1]
    pre_acts = (
        jnp.einsum("krd,kdf->krf", inputs, encoder, preferred_element_type=jnp.float32)
        + enc_bias[:, None, :]
    )
    block_ids = offset // BLOCK + jnp.arange(local_width // BLOCK, dtype=jnp.int32)
    block_masks = []
    for layer_id in layer_ids:
        listed = lax.dynamic_index_in_dim(active, layer_id, 0, keepdims=False)
        listed_hit = jnp.any(listed[:, :, None] == block_ids[None, None, :], axis=1).astype(
            jnp.float32
        )
        spread = jnp.broadcast_to(
            listed_hit[:, None, :, None], (listed_hit.shape[0], tok_dev, listed_hit.shape[1], BLOCK)
        )
        block_masks.append(spread.reshape(tokens, local_width))
    block_keep = jnp.stack(block_masks)
    positive = jnp.maximum(pre_acts, 0.0)
    feature_codes = (block_keep * positive * positive).astype(jnp.bfloat16)
    recon, errors_all, back_codes = exchange(
        feature_codes, decoder, resid_out, layer_count, dp_count
    )
    pair_slots = jnp.arange(decoder.shape[0], dtype=jnp.int32)
    second = pair_slots >= LAYERS - fold_side
    sources = second.astype(jnp.int32)
    decoded_into = jnp.where(second, pair_slots - 1, fold_side + pair_slots).astype(jnp.int32)
    grad_decoder = decoder_grad(
        feature_codes, errors_all, sources, decoded_into, decoder.shape[0]
    )
    grad_encoder, grad_bias = encoder_grad(inputs, back_codes, block_keep, positive)
    return (recon, grad_encoder, grad_bias, grad_decoder)


def solution(mesh):
    in_specs = (
        P(None, "dp", None),
        P(None, ("layer", "dp"), None),
        P(None, None, ("layer", "dp")),
        P(None, ("layer", "dp")),
        P(None, ("layer", "dp"), None),
        P(),
    )
    out_specs = (
        P(None, ("layer", "dp"), None),
        P(None, None, ("layer", "dp")),
        P(None, ("layer", "dp")),
        P(None, ("layer", "dp"), None),
    )
    return jax.shard_map(
        per_device, mesh=mesh, in_specs=in_specs, out_specs=out_specs, check_vma=False
    )
```

```python
import functools

import jax
import jax.numpy as jnp
from jax import lax
from jax.experimental import pallas as pl
from jax.experimental.pallas import tpu as pltpu
from jax.sharding import PartitionSpec as P

FEAT = 16384
BLOCK = 128
LAYERS = 4
MESH = pl.DeviceIdType.MESH
VMEM_LIMIT = 63 * 1000 * 1000


def remote(src, dst, send_sem, recv_sem, layer, dp):
    return pltpu.make_async_remote_copy(
        src_ref=src,
        dst_ref=dst,
        send_sem=send_sem,
        recv_sem=recv_sem,
        device_id=(layer, dp),
        device_id_type=MESH,
    )


def greet(layer, dp, dp_count, bits):
    barrier = pltpu.get_barrier_semaphore()
    for hop in range(1, dp_count):
        pl.semaphore_signal(
            barrier, inc=1, device_id=(layer, lax.rem(dp + hop, dp_count)), device_id_type=MESH
        )
    for bit in bits:
        pl.semaphore_signal(
            barrier, inc=1, device_id=(flip(layer, bit), dp), device_id_type=MESH
        )
    return barrier, dp_count - 1 + len(bits)


def bit_of(value, bit):
    return (value // (1 << bit)) % 2


def flip(value, bit):
    return value + (1 - 2 * bit_of(value, bit)) * (1 << bit)


def spread_bits(base, bits, count):
    for place, bit in enumerate(bits):
        base = base + (((count >> place) & 1) - bit_of(base, bit)) * (1 << bit)
    return base


def gather_kernel(layer_count, dp_count, x_ref, g_ref, hold, send_sem, recv_sem, near_sem, out_sem):
    layer, dp = lax.axis_index("layer"), lax.axis_index("dp")
    group = layer_count // 2
    halves = x_ref.shape[1]
    nbits = group.bit_length() - 1
    side = layer // group
    bits = list(range(nbits - 1, -1, -1))
    barrier, greeted = greet(layer, dp, dp_count, bits)
    mine = layer % group
    near = []
    for slot in range(2):
        layer_id = side + slot * (LAYERS - 1 - 2 * side)
        copy = pltpu.make_async_copy(
            x_ref.at[layer_id], hold.at[slot, dp], near_sem.at[slot]
        )
        copy.start()
        near.append(copy)
    pl.semaphore_wait(barrier, greeted)

    def piece(ref, source, index):
        return ref.at[index // halves, source, index % halves]

    copies = {}
    my_slot = mine // halves
    own = x_ref.at[side + my_slot * (LAYERS - 1 - 2 * side), mine % halves]
    for hop in range(1, dp_count):
        copies[hop, 0] = remote(
            own, piece(hold, dp, mine), send_sem.at[hop, 0], recv_sem.at[hop, 0],
            layer, lax.rem(dp + hop, dp_count),
        )
        copies[hop, 0].start()
    for step, bit in enumerate(bits):
        for hop in range(1, dp_count):
            source = lax.rem(dp + dp_count - hop, dp_count)
            arrived = [0] if step == 0 else range(1 << (step - 1), 1 << step)
            for index in arrived:
                copies[hop, index].wait_recv()
            for count in range(1 << step):
                index = spread_bits(mine, bits[:step], count)
                slot = (1 << step) + count
                block = piece(hold, source, index)
                copies[hop, slot] = remote(
                    block, block, send_sem.at[hop, slot], recv_sem.at[hop, slot],
                    flip(layer, bit), dp,
                )
                copies[hop, slot].start()
    for hop in range(1, dp_count):
        for index in range(group // 2, group):
            copies[hop, index].wait_recv()
    for copy in near:
        copy.wait()
    out = pltpu.make_async_copy(hold, g_ref, out_sem)
    out.start()
    for copy in copies.values():
        copy.wait_send()
    out.wait()


def gather_inputs(resid_in, layer_count, dp_count):
    layers, tok_dev, width = resid_in.shape
    group = layer_count // 2
    halves = group // 2
    rows = tok_dev // halves
    x = resid_in.reshape(layers, halves, rows, width)
    shape = (2, dp_count, halves, rows, width)
    out = pl.pallas_call(
        functools.partial(gather_kernel, layer_count, dp_count),
        out_shape=jax.ShapeDtypeStruct(shape, resid_in.dtype),
        in_specs=[pl.BlockSpec(memory_space=pltpu.VMEM)],
        out_specs=pl.BlockSpec(memory_space=pl.ANY),
        scratch_shapes=[
            pltpu.VMEM(shape, resid_in.dtype),
            pltpu.SemaphoreType.DMA((dp_count, group)),
            pltpu.SemaphoreType.DMA((dp_count, group)),
            pltpu.SemaphoreType.DMA((2,)),
            pltpu.SemaphoreType.DMA,
        ],
        compiler_params=pltpu.CompilerParams(
            collective_id=0, has_side_effects=True, vmem_limit_bytes=32 * 1000 * 1000
        ),
        name="gather_inputs",
    )(x)
    return out.reshape(2, dp_count * tok_dev, width)


def exchange_kernel(
    layer_count, dp_count, codes_ref, dec_ref, target_ref, recon_ref, err_out, back_ref,
    weights, part, arrivals, err, zsend, zrecv, zall, acc,
    load_sem, rs_send, rs_recv, z_send, z_recv, g_send, g_recv, ag_send, ag_recv, out_sem,
):
    layer, dp = lax.axis_index("layer"), lax.axis_index("dp")
    nbits = layer_count.bit_length() - 1
    side = layer // (layer_count // 2)
    pairs, width = dec_ref.shape[0], dec_ref.shape[2]
    rows = part.shape[2]
    share = target_ref.shape[1]
    f32, bf16 = jnp.float32, jnp.bfloat16

    def load(pair):
        return pltpu.make_async_copy(dec_ref.at[pair], weights.at[pair], load_sem.at[pair])

    for pair in range(LAYERS - 1):
        load(pair).start()
    for pair in range(LAYERS - 1, pairs):
        load(pair).start()
    barrier, greeted = greet(layer, dp, dp_count, range(nbits))
    tile = 512 if width % 512 == 0 else 128
    orders = []
    for target in range(LAYERS):
        upper = list(range(nbits - 1, 0, -1))
        orders.append([0] + (upper if target % 2 else upper[::-1]))
    copies = {}

    def add_pair(slot, pair, fresh):
        load(pair).wait()

        def body(step, carry):
            columns = pl.ds(pl.multiple_of(step * tile, tile), tile)
            value = jnp.dot(
                codes_ref[slot], weights[pair, :, columns], preferred_element_type=f32
            )
            if fresh:
                acc[:, columns] = value
            else:
                acc[:, columns] += value
            return carry

        lax.fori_loop(0, width // tile, body, 0)

    def pull_pair(target, slot, pair, fresh):
        deep = min(256, weights.shape[1])

        def body(step, carry):
            features = pl.ds(pl.multiple_of(step * deep, deep), deep)
            value = lax.dot_general(
                err[target].reshape(acc.shape),
                weights[pair, features, :],
                (((1,), (1,)), ((), ())),
                preferred_element_type=f32,
            )
            if fresh:
                back_ref[slot, :, features] = value
            else:
                back_ref[slot, :, features] += value
            return carry

        lax.fori_loop(0, weights.shape[1] // deep, body, 0)

    def pull(target):
        if target == 0:
            pl.when(side == 0)(lambda: pull_pair(0, 0, 0, True))
        elif target == 1:
            pl.when(side == 0)(lambda: pull_pair(1, 0, 1, False))
            pl.when(side == 1)(lambda: pull_pair(1, 0, 0, True))
        else:
            pull_pair(target, 0, target - side, False)
        if target == LAYERS - 2:
            pl.when(side == 1)(lambda: pull_pair(target, 1, target + 1, True))
        elif target == LAYERS - 1:
            pl.when(side == 1)(lambda: pull_pair(target, 1, target + 1, False))
            pl.when(side == 0)(lambda: pull_pair(target, 1, target + 1, True))

    def decode(target):
        def first():
            add_pair(0, target - side, True)

        if target == 0:
            pl.when(side == 0)(first)

            @pl.when(side != 0)
            def _():
                acc[...] = jnp.zeros_like(acc)
        else:
            first()
        if target >= LAYERS - 2:
            def second():
                add_pair(1, target + 1, False)

            if target == LAYERS - 2:
                pl.when(side == 1)(second)
            else:
                second()
        part[target] = acc[...].reshape(part.shape[1:]).astype(bf16)

    def halve_send(target, stage):
        order = orders[target]
        bit = order[stage]
        partner = flip(layer, bit)
        rest = order[stage + 1:]
        for count in range(1 << len(rest)):
            block = spread_bits(partner, rest, count)
            slot = (1 << len(rest)) - 1 + count
            copy = remote(
                part.at[target, block], arrivals.at[target, slot],
                rs_send.at[target, slot], rs_recv.at[target, slot], partner, dp,
            )
            copy.start()
            copies["rs", target, slot] = copy

    def halve_take(target, stage):
        order = orders[target]
        rest = order[stage + 1:]
        for count in range(1 << len(rest)):
            slot = (1 << len(rest)) - 1 + count
            copies["rs", target, slot].wait_recv()
            block = spread_bits(layer, rest, count)
            total = part[target, block].astype(f32) + arrivals[target, slot].astype(f32)
            if stage < nbits - 1:
                part[target, block] = total.astype(bf16)
            else:
                for place in range(dp_count):
                    zsend[target, place] = total[place * share:(place + 1) * share].astype(bf16)

    def peers():
        for hop in range(1, dp_count):
            yield hop, lax.rem(dp + hop, dp_count)

    def swap_send(target):
        for hop, peer in peers():
            copy = remote(
                zsend.at[target, peer], zrecv.at[target, hop],
                z_send.at[target, hop], z_recv.at[target, hop], layer, peer,
            )
            copy.start()
            copies["z", target, hop] = copy

    def finish(target):
        total = zsend[target, dp].astype(f32)
        for hop in range(1, dp_count):
            copies["z", target, hop].wait_recv()
            total = total + zrecv[target, hop].astype(f32)
        recon_ref[target] = total.astype(bf16)
        zall[target, dp] = (total - target_ref[target].astype(f32)).astype(bf16)
        for hop, peer in peers():
            copy = remote(
                zall.at[target, dp], zall.at[target, dp],
                g_send.at[target, hop], g_recv.at[target, hop], layer, peer,
            )
            copy.start()
            copies["g", target, hop] = copy

    def assemble(target):
        for hop in range(1, dp_count):
            copies["g", target, hop].wait_recv()
        err[target, layer] = jnp.concatenate(
            [zall[target, place].astype(f32) for place in range(dp_count)], axis=0
        ).astype(bf16)

    def double_send(target, step):
        order = orders[target][::-1]
        bit = order[step]
        for count in range(1 << step):
            block = spread_bits(layer, order[:step], count)
            slot = (1 << step) - 1 + count
            copy = remote(
                err.at[target, block], err.at[target, block],
                ag_send.at[target, slot], ag_recv.at[target, slot], flip(layer, bit), dp,
            )
            copy.start()
            copies["ag", target, slot] = copy

    def double_take(target, step):
        for count in range(1 << step):
            copies["ag", target, (1 << step) - 1 + count].wait_recv()

    def run(target, stage):
        if stage == 0:
            decode(target)
            if target == 0:
                pl.semaphore_wait(barrier, greeted)
            halve_send(target, 0)
        elif stage <= nbits:
            halve_take(target, stage - 1)
            if stage < nbits:
                halve_send(target, stage)
            else:
                swap_send(target)
        elif stage == nbits + 1:
            finish(target)
        elif stage == nbits + 2:
            assemble(target)
            double_send(target, 0)
        else:
            step = stage - nbits - 3
            double_take(target, step)
            if step < nbits - 1:
                double_send(target, step + 1)
            else:
                copy = pltpu.make_async_copy(err.at[target], err_out.at[target], out_sem.at[target])
                copy.start()
                copies["out", target, 0] = copy

    last = 2 * nbits + 2
    for wave in range(last + LAYERS):
        for target in range(LAYERS - 1, -1, -1):
            if 0 <= wave - target <= last:
                run(target, wave - target)
        if 0 <= wave - last < LAYERS:
            pull(wave - last)
    for key, copy in copies.items():
        if key[0] == "out":
            copy.wait()
        else:
            copy.wait_send()


def exchange(codes, decoder, targets, layer_count, dp_count):
    tokens = codes.shape[1]
    pairs, local_width, width = decoder.shape
    rows = tokens // layer_count
    share = rows // dp_count
    bf16 = jnp.bfloat16
    dma = pltpu.SemaphoreType.DMA
    recon, errors, back = pl.pallas_call(
        functools.partial(exchange_kernel, layer_count, dp_count),
        out_shape=[
            jax.ShapeDtypeStruct((LAYERS, share, width), bf16),
            jax.ShapeDtypeStruct((LAYERS, layer_count, rows, width), bf16),
            jax.ShapeDtypeStruct((2, tokens, local_width), jnp.float32),
        ],
        in_specs=[
            pl.BlockSpec(memory_space=pltpu.VMEM),
            pl.BlockSpec(memory_space=pl.ANY),
            pl.BlockSpec(memory_space=pltpu.VMEM),
        ],
        out_specs=[
            pl.BlockSpec(memory_space=pltpu.VMEM),
            pl.BlockSpec(memory_space=pl.ANY),
            pl.BlockSpec(memory_space=pltpu.VMEM),
        ],
        scratch_shapes=[
            pltpu.VMEM((pairs, local_width, width), bf16),
            pltpu.VMEM((LAYERS, layer_count, rows, width), bf16),
            pltpu.VMEM((LAYERS, layer_count - 1, rows, width), bf16),
            pltpu.VMEM((LAYERS, layer_count, rows, width), bf16),
            pltpu.VMEM((LAYERS, dp_count, share, width), bf16),
            pltpu.VMEM((LAYERS, dp_count, share, width), bf16),
            pltpu.VMEM((LAYERS, dp_count, share, width), bf16),
            pltpu.VMEM((tokens, width), jnp.float32),
            dma((pairs,)),
            dma((LAYERS, layer_count - 1)),
            dma((LAYERS, layer_count - 1)),
            dma((LAYERS, dp_count)),
            dma((LAYERS, dp_count)),
            dma((LAYERS, dp_count)),
            dma((LAYERS, dp_count)),
            dma((LAYERS, layer_count - 1)),
            dma((LAYERS, layer_count - 1)),
            dma((LAYERS,)),
        ],
        compiler_params=pltpu.CompilerParams(
            collective_id=1, has_side_effects=True, vmem_limit_bytes=VMEM_LIMIT
        ),
        name="decode_exchange",
    )(codes, decoder, targets)
    return recon, errors.reshape(LAYERS, tokens, width), back


def half_width(width):
    return width // 2 if width % 256 == 0 else width


def grad_decoder_kernel(side_ref, codes_ref, err_ref, out_ref, turned):
    @pl.when(pl.program_id(1) == 0)
    def _():
        turned[...] = codes_ref[0].T

    width = err_ref.shape[2]
    tile = 256 if width % 256 == 0 else 128
    for first in range(0, width, tile):
        out_ref[0, :, first:first + tile] = jnp.dot(
            turned[...], err_ref[0, :, first:first + tile], preferred_element_type=jnp.float32
        ).astype(out_ref.dtype)


def decoder_grad(codes, errors, side, pairs):
    tokens, local_width = codes.shape[1:]
    width = errors.shape[2]
    block = half_width(width)

    def source(pair, side_ref):
        return (pair + side_ref[0]) // LAYERS

    def target(pair, side_ref):
        return pair + side_ref[0] - source(pair, side_ref) * (1 + side_ref[0])

    return pl.pallas_call(
        grad_decoder_kernel,
        out_shape=jax.ShapeDtypeStruct((pairs, local_width, width), jnp.bfloat16),
        grid_spec=pltpu.PrefetchScalarGridSpec(
            num_scalar_prefetch=1,
            grid=(pairs, width // block),
            in_specs=[
                pl.BlockSpec((1, tokens, local_width), lambda p, d, s: (source(p, s), 0, 0)),
                pl.BlockSpec((1, tokens, block), lambda p, d, s: (target(p, s), 0, d)),
            ],
            out_specs=pl.BlockSpec((1, local_width, block), lambda p, d, s: (p, 0, d)),
            scratch_shapes=[pltpu.VMEM((local_width, tokens), codes.dtype)],
        ),
        name="decoder_grad",
    )(side, codes, errors)


def grad_encoder_kernel(x_ref, back_ref, keep_ref, positive_ref, grad_ref, bias_ref, back_pre):
    slot = pl.program_id(0)

    @pl.when(pl.program_id(1) == 0)
    def _():
        value = (back_ref[0] * keep_ref[0] * (2.0 * positive_ref[0])).astype(jnp.bfloat16)
        back_pre[...] = value
        bias_ref[pl.ds(slot, 1), :] = jnp.sum(value.astype(jnp.float32), axis=0, keepdims=True)

    turned = x_ref[0].T
    tile = min(256, back_pre.shape[1])
    for first in range(0, back_pre.shape[1], tile):
        grad_ref[0, :, first:first + tile] = jnp.dot(
            turned, back_pre[:, first:first + tile], preferred_element_type=jnp.float32
        ).astype(grad_ref.dtype)


def encoder_grad(inputs, back, keep, positive):
    slots, tokens, width = inputs.shape
    local_width = back.shape[2]
    block = half_width(width)
    whole = pl.BlockSpec((1, tokens, local_width), lambda k, d: (k, 0, 0))
    return pl.pallas_call(
        grad_encoder_kernel,
        out_shape=[
            jax.ShapeDtypeStruct((slots, width, local_width), jnp.bfloat16),
            jax.ShapeDtypeStruct((slots, local_width), jnp.float32),
        ],
        grid=(slots, width // block),
        in_specs=[pl.BlockSpec((1, tokens, block), lambda k, d: (k, 0, d)), whole, whole, whole],
        out_specs=[
            pl.BlockSpec((1, block, local_width), lambda k, d: (k, d, 0)),
            pl.BlockSpec((slots, local_width), lambda k, d: (0, 0)),
        ],
        scratch_shapes=[pltpu.VMEM((tokens, local_width), jnp.bfloat16)],
        name="encoder_grad",
    )(inputs, back, keep, positive)


def per_device(resid_in, resid_out, encoder, enc_bias, decoder, active):
    tok_dev = resid_in.shape[1]
    local_width = encoder.shape[2]
    layer_count = lax.axis_size("layer")
    dp_count = lax.axis_size("dp")
    device_rank = lax.axis_index("layer") * dp_count + lax.axis_index("dp")
    first_column = device_rank * local_width
    fold_side = first_column // FEAT
    offset = first_column - fold_side * FEAT
    layer_ids = [fold_side, LAYERS - 1 - fold_side]
    inputs = gather_inputs(resid_in, layer_count, dp_count)
    tokens = inputs.shape[1]
    pre_acts = (
        jnp.einsum("krd,kdf->krf", inputs, encoder, preferred_element_type=jnp.float32)
        + enc_bias[:, None, :]
    )
    block_ids = offset // BLOCK + jnp.arange(local_width // BLOCK, dtype=jnp.int32)
    block_masks = []
    for layer_id in layer_ids:
        listed = lax.dynamic_index_in_dim(active, layer_id, 0, keepdims=False)
        listed_hit = jnp.any(listed[:, :, None] == block_ids[None, None, :], axis=1).astype(
            jnp.float32
        )
        spread = jnp.broadcast_to(
            listed_hit[:, None, :, None], (listed_hit.shape[0], tok_dev, listed_hit.shape[1], BLOCK)
        )
        block_masks.append(spread.reshape(tokens, local_width))
    block_keep = jnp.stack(block_masks)
    positive = jnp.maximum(pre_acts, 0.0)
    feature_codes = (block_keep * positive * positive).astype(jnp.bfloat16)
    recon, errors_all, back_codes = exchange(
        feature_codes, decoder, resid_out, layer_count, dp_count
    )
    side = fold_side.astype(jnp.int32).reshape(1)
    grad_decoder = decoder_grad(feature_codes, errors_all, side, decoder.shape[0])
    grad_encoder, grad_bias = encoder_grad(inputs, back_codes, block_keep, positive)
    return (recon, grad_encoder, grad_bias, grad_decoder)


def solution(mesh):
    in_specs = (
        P(None, "dp", None),
        P(None, ("layer", "dp"), None),
        P(None, None, ("layer", "dp")),
        P(None, ("layer", "dp")),
        P(None, ("layer", "dp"), None),
        P(),
    )
    out_specs = (
        P(None, ("layer", "dp"), None),
        P(None, None, ("layer", "dp")),
        P(None, ("layer", "dp")),
        P(None, ("layer", "dp"), None),
    )
    return jax.shard_map(
        per_device, mesh=mesh, in_specs=in_specs, out_specs=out_specs, check_vma=False
    )
```
